256 devices in a mesh: leaf: 2 (over core), row: 16 (over z, x_lo), col: 8 (over y, x_hi).
Axes of the slice: x: 4 (x_hi: 2, x_lo: 2; x = x_hi * 2 + x_lo), y: 4, z: 8, core: 2. Of those that a mesh axis runs over, the one named last changes fastest.
Arguments:
- child_tiles: float32 [1024, 64, 4096], P(('leaf', 'row'), None, 'col'), may hold values from -0.078125 to 0.078125
- block_mask: int32 [1024, 64], P(('leaf', 'row'), 'col'), may hold values 0 or 1
- destination: int32 [1024, 1], P(('leaf', 'row')), may hold values from 0 to 31; in each aligned block of 32 rows (0 to 31, 32 to 63, ...) at most 2 rows name the same one
Outputs:
- r_top: float32 [2, 128, 4096], P('leaf', None, 'col')
The draws below stay inside these ranges and needn't reach their ends.
Inputs may be any that keep to these rules, and one draw needn't show every extreme that they name: Among the tiles of one device, no destination is named more than 2 times, a bound that some block reaches.
All inputs are finite; a program needn't handle non-finite values. No bound on the sum of `block_mask` on one device may be relied on, other than what follows from the above.
Results may differ from the reference program's by a relative error of at most 0.0003.
Values sent between devices are 32-bit elements; how exact they have to be, the bound alone decides.
A program may use at most 64 MiB of HBM per device.

```python
import math
import jax
import jax.numpy as jnp
import numpy as np
from jax import lax

BLOCK_EDGE = 64
PARENT_COLUMNS = 4096
CAP = 2
FRONTS = 2
NDEST = 32
TILES_DEV = 32
TILES = 1024
NBLOCKS = 64
COLUMN_BLOCKS = 8
ELIMINATED_COLS = 128
N_LEAF = 2
N_ROW = 16
N_COL = 8


def place_ends(result, own_key, least, high):
    index_at = [jax.random.randint(jax.random.fold_in(own_key, axis), (), 0, length) for axis, length in enumerate(result.shape)]
    widest = result.shape.index(max(result.shape))
    next_to = index_at[:widest] + [(index_at[widest] + 1) % result.shape[widest]] + index_at[widest + 1:]
    return result.at[tuple(index_at)].set(least).at[tuple(next_to)].set(high)


def level_of(stream_key, extent, pieces, least, largest):
    factor_of = 1.0
    for position, shards_of in pieces:
        heights = jax.random.uniform(jax.random.fold_in(jax.random.fold_in(stream_key, 6), position), (shards_of,), jnp.float32, least / len(pieces), largest / len(pieces))
        factor_of = factor_of * jnp.repeat(jnp.exp(heights), extent[position] // shards_of).reshape((-1,) + (1,) * (len(extent) - 1 - position))
    return factor_of


def assign_block(stream_key, own, number, rows, number_of, top, reach, slope):
    order = jax.random.permutation(stream_key, number_of)
    crowded, usual = shares(number_of, rows * top, reach, slope, True), shares(number_of, rows * top, reach, slope, False)
    places = jnp.arange(number_of)

    def named(sizes, turn):
        used = int((sizes > 0).sum())
        fixed = max(1, used // 4)
        moved = fixed + (places - fixed + turn * (used - fixed)) % max(1, number_of - fixed)
        return jnp.zeros((number_of,), jnp.int32).at[order[jnp.where(places < fixed, places, moved)]].set(jnp.asarray(sizes, jnp.int32))

    sizes = jnp.where(number % 4 == 0, named(crowded, number // 4), named(usual, number - number // 4 - 1))
    mixed = jax.random.permutation(jax.random.fold_in(own, 3), number_of)
    donor, sink = mixed[0:number_of // 2 * 2:2], mixed[1:number_of // 2 * 2:2]
    room = jnp.minimum(sizes[donor] - 1, reach - sizes[sink]) // 2
    room = jnp.where((donor == order[0]) | (sink == order[0]) | (sizes[sink] == 0), 0, jnp.maximum(room, 0))
    moved = jax.random.randint(jax.random.fold_in(own, 4), (number_of // 2,), 0, 1 << 20) % (room + 1)
    sizes = sizes.at[donor].add(-moved).at[sink].add(moved)
    items = jnp.searchsorted(jnp.cumsum(sizes), jnp.arange(rows * top), side="right").astype(jnp.int32)
    table = items.reshape(top, rows).T
    table = table[jax.random.permutation(jax.random.fold_in(own, 1), rows)]
    turn = jax.random.randint(jax.random.fold_in(own, 2), (rows, 1), 0, top)
    return jnp.take_along_axis(table, (jnp.arange(top)[None, :] + turn) % top, axis=1)


def shares(number_of, total, bound, lean, full):
    loads = [(1 << 20) // math.isqrt(rank ** lean) + 1 for rank in range(1, number_of + 1)]
    largest = bound if full else min(bound, max(-(-total // number_of), total * loads[0] // sum(loads)))
    least = 1 if total - largest >= number_of - 1 else 0
    given, rest = [largest] + [least] * (number_of - 1), total - largest - least * (number_of - 1)
    while rest > 0:
        candidates = [i for i in range(1, number_of) if given[i] < largest] or [i for i in range(1, number_of) if given[i] < bound]
        mass, budget = sum([loads[i] for i in candidates]), rest
        for i in candidates:
            extra = min(bound - given[i], max(1, budget * loads[i] // mass), rest)
            given[i] = given[i] + extra
            rest = rest - extra
    return np.array(given)


def normal_values(key, dims, deviation, most, shards=(), kind=jnp.bfloat16):
    result = deviation * jax.random.normal(key, dims, jnp.float32)
    if shards:
        result = result * level_of(key, dims, shards, -0.22, 0.18)
    return jnp.clip(result, -most, most).astype(kind)


def setup_inputs(seed: int = 0) -> dict:
    arg_keys = jax.random.split(jax.random.key(seed), 4)
    child_tiles = normal_values(arg_keys[0], (TILES, BLOCK_EDGE, PARENT_COLUMNS), ((TILES_DEV * N_ROW * BLOCK_EDGE) ** -0.5), 0.078125, ((0, 32), (2, 8)), jnp.float32)
    block_mask = place_ends((jax.random.randint(arg_keys[1], (TILES, NBLOCKS), 0, 4) < 3).astype(jnp.int32), jax.random.fold_in(arg_keys[1], 1), 0, 1)
    destination_keys = jax.random.split(jax.random.fold_in(arg_keys[2], 1), TILES // TILES_DEV)
    destination_turns = jax.random.permutation(jax.random.fold_in(arg_keys[2], 3), TILES // TILES_DEV)
    destination = jax.vmap(lambda own, number: assign_block(jax.random.fold_in(arg_keys[2], 2), own, number, TILES_DEV, NDEST, 1, CAP, 1))(destination_keys, destination_turns).reshape((TILES, 1))
    return dict(child_tiles=child_tiles, block_mask=block_mask, destination=destination)


def front_top(child_tiles, block_mask, destination, front_id):
    per_front = NDEST // FRONTS
    owner_front = destination[:, 0] // per_front
    outside = (owner_front != front_id).astype(jnp.int32)
    picked_count = min(TILES, N_LEAF * N_ROW * per_front * CAP)
    order = jnp.argsort(outside, stable=True)[:picked_count].astype(jnp.int32)
    inside = (owner_front[order] == front_id).astype(jnp.float32)
    chosen = child_tiles[order].reshape(picked_count, BLOCK_EDGE, NBLOCKS, BLOCK_EDGE)
    masks = block_mask[order].astype(jnp.float32)
    chosen = chosen * masks[:, None, :, None] * inside[:, None, None, None]
    stacked_tiles = chosen.reshape(picked_count * BLOCK_EDGE, N_COL, COLUMN_BLOCKS, BLOCK_EDGE)
    stacked_tiles = stacked_tiles.transpose(0, 2, 1, 3).reshape(picked_count * BLOCK_EDGE, PARENT_COLUMNS)
    leading_rows = stacked_tiles[:, :ELIMINATED_COLS]
    orthogonal_factor, upper_leading = jnp.linalg.qr(leading_rows)
    diagonal_signs = jnp.sign(jnp.diagonal(upper_leading))
    upper_remainder = jnp.dot(orthogonal_factor.T, stacked_tiles[:, ELIMINATED_COLS:], precision=lax.Precision.HIGHEST)
    upper_eliminated = diagonal_signs[:, None] * jnp.concatenate([upper_leading, upper_remainder], axis=1)
    return upper_eliminated.reshape(ELIMINATED_COLS, COLUMN_BLOCKS, N_COL, BLOCK_EDGE).transpose(0, 2, 1, 3).reshape(ELIMINATED_COLS, PARENT_COLUMNS)

def reference(child_tiles, block_mask, destination):

    def one_front(front_id):
        return front_top(child_tiles, block_mask, destination, front_id)
    return lax.map(one_front, jnp.arange(FRONTS, dtype=jnp.int32))
```

```python
import jax
import jax.numpy as jnp
from jax import lax
from jax.sharding import PartitionSpec as P

FRONTS = 2


def per_device(child_tiles, block_mask, destination):
    tile_count, edge, columns_dev = child_tiles.shape
    blocks_dev = columns_dev // edge
    col = lax.axis_index("col")
    per_front = lax.axis_size("row")
    mask = block_mask.astype(jnp.float32)
    rows = tile_count * edge
    tiles = child_tiles.reshape(rows, columns_dev)
    own = tiles[:, :edge] * jnp.repeat(mask[:, 0], edge)[:, None]
    panel = jnp.concatenate([jnp.where(col == k, own, 0.0) for k in range(2)], axis=1)
    panel = lax.psum(panel, "col")
    front = jnp.repeat(destination[:, 0] // per_front, edge)[:, None]
    left = jnp.concatenate([jnp.where(front == f, panel, 0.0) for f in range(FRONTS)], axis=1)
    masked = (tiles.reshape(tile_count, edge, blocks_dev, edge) * mask[:, None, :, None]).reshape(rows, columns_dev)
    dot = lambda a, b: lax.dot_general(a, b, (((0,), (0,)), ((), ())), precision=lax.Precision.HIGHEST)
    sums = jnp.concatenate([dot(left, masked), dot(left, panel)], axis=1)
    sums = lax.psum_scatter(sums, "leaf", scatter_dimension=0, tiled=True)
    sums = lax.psum(sums, "row")
    cross, gram = sums[:, :columns_dev], sums[:, columns_dev:]
    lower = jnp.linalg.cholesky(gram)
    top = lax.linalg.triangular_solve(lower, cross, left_side=True, lower=True)
    col_count = lax.axis_size("col")
    place = jnp.repeat(jnp.arange(blocks_dev) * col_count + col, edge)
    line = jnp.arange(2 * edge) // edge
    return jnp.where(place[None, :] >= line[:, None], top, 0.0)[None]


def solution(mesh):
    in_specs = (
        P(("leaf", "row"), None, "col"),
        P(("leaf", "row"), "col"),
        P(("leaf", "row"), None),
    )
    return jax.shard_map(
        per_device, mesh=mesh, in_specs=in_specs, out_specs=P("leaf", None, "col"), check_vma=False
    )
```

```python
import functools

import jax
import jax.numpy as jnp
from jax import lax
from jax.experimental import pallas as pl
from jax.experimental.pallas import tpu as pltpu
from jax.sharding import PartitionSpec as P

MESH = pl.DeviceIdType.MESH
HIGH = lax.Precision.HIGHEST
EDGE = 64
PAIRS = 8
RETURNED = (0, 3, 5)
CROSSED_FIRST = (1, 4, 6)
LAG = 2


def one_of(i, members):
    hit = i == members[0]
    for m in members[1:]:
        hit = jnp.logical_or(hit, i == m)
    return hit


def gather_kernel(tiles, mask, dest, out, wide, pan, acc, got, front, part, full, load_sem, send_sem, recv_sem, leaf_sem, rs_sem, ag_sem):
    leaf = lax.axis_index("leaf")
    row = lax.axis_index("row")
    col = lax.axis_index("col")
    y = col // 2
    mine = col % 2
    other = 1 - mine
    rows_n = lax.axis_size("row")

    def at(y_to, x_to):
        return (leaf, row, lax.rem(y_to + 4, 4) * 2 + x_to)

    up, down, across = at(y + 1, mine), at(y - 1, mine), at(y, other)
    peer = lambda j: (leaf, lax.rem(row + j, rows_n), col)
    partner = (1 - leaf, row, col)

    lanes = 128
    loads = []
    for b in range(4):
        span = pl.ds(b * lanes, lanes)
        loads.append(pltpu.make_async_copy(tiles.at[:, :, span], wide.at[:, :, span], load_sem.at[b]))
        loads[-1].start()

    barrier = pltpu.get_barrier_semaphore()
    targets = [up, down, across, partner] + [peer(j) for j in range(1, 16)]
    for t in targets:
        pl.semaphore_signal(barrier, inc=1, device_id=t, device_id_type=MESH)

    expand = (lax.broadcasted_iota(jnp.int32, (8, 512), 1) // EDGE == lax.broadcasted_iota(jnp.int32, (8, 512), 0)).astype(jnp.float32)
    maskw = jnp.dot(mask[...].astype(jnp.float32), expand, preferred_element_type=jnp.float32)
    in_first = (dest[...] < 16).astype(jnp.float32)
    place = (lax.broadcasted_iota(jnp.int32, (32, 2048), 1) // EDGE == lax.broadcasted_iota(jnp.int32, (32, 2048), 0)).astype(jnp.float32)
    first = jnp.sum(place * in_first, axis=0, keepdims=True)
    for k in range(PAIRS):
        front[k] = jnp.broadcast_to(first[:, k * 256:(k + 1) * 256], (8, 256))
    for t in range(32):
        got[t] = jnp.broadcast_to(maskw[t:t + 1], (8, 512))

    def copy_of(p, c, way, to):
        return pltpu.make_async_remote_copy(
            src_ref=pan.at[p, c], dst_ref=pan.at[p, c], send_sem=send_sem.at[way, p, c],
            recv_sem=recv_sem.at[p, c], device_id=to, device_id_type=MESH)

    def forward(i, d, act):
        c = 2 * i + d
        step = y if d == 0 else lax.rem(4 - y, 4)
        ahead, back = (up, down) if d == 0 else (down, up)
        returned, crossed = one_of(i, RETURNED), one_of(i, CROSSED_FIRST)
        del back

        @pl.when(step < 3)
        def _():
            act(copy_of(mine, c, 0, ahead))

        later = jnp.logical_and(step > 0, jnp.logical_not(crossed))
        now = jnp.logical_and(step == 0, jnp.logical_not(returned))

        @pl.when(jnp.logical_or(later, now))
        def _():
            act(copy_of(mine, c, 1, across))

    def forward_other(i, d, act):
        c = 2 * i + d
        step = y if d == 0 else lax.rem(4 - y, 4)
        ahead, back = (up, down) if d == 0 else (down, up)
        returned, crossed = one_of(i, RETURNED), one_of(i, CROSSED_FIRST)

        @pl.when(jnp.logical_and(crossed, step < 3))
        def _():
            act(copy_of(other, c, 0, ahead))

        @pl.when(jnp.logical_and(returned, step == 1))
        def _():
            act(copy_of(other, c, 0, back))

    start = lambda cp: cp.start()
    drain = lambda cp: cp.wait_send()

    loads[0].wait()
    pl.semaphore_wait(barrier, len(targets))

    @pl.when(y == 0)
    def _():
        def pack(i, carry):
            for d in range(2):
                c = 2 * i + d
                two = []
                for t in range(2):
                    tile = 2 * c + t
                    two.append(wide[tile, :, 0:lanes] * got[tile, 0:1, 0:lanes])
                flat = jnp.concatenate(two, axis=0)
                pan[mine, c] = flat.T[0:EDGE, :]
                forward(i, d, start)
            return carry

        lax.fori_loop(0, PAIRS, pack, 0)

    acc[...] = jnp.zeros_like(acc)
    for b in range(1, 4):
        loads[b].wait()

    def step_fn(i, carry):
        @pl.when(jnp.logical_and(i < PAIRS, y > 0))
        def _():
            for d in range(2):
                copy_of(mine, 2 * i + d, 0, up).wait_recv()
                forward(i, d, start)

        @pl.when(i >= LAG)
        def _():
            k = i - LAG
            for d in range(2):
                copy_of(other, 2 * k + d, 0, up).wait_recv()
                forward_other(k, d, start)
            right = []
            for t in range(4):
                tile = 4 * k + t
                right.append(wide[tile] * got[tile, 0:1, :])
            right = jnp.concatenate(right, axis=0)
            left = jnp.concatenate(
                [jnp.concatenate([pan[p, 2 * k], pan[p, 2 * k + 1]], axis=1) for p in range(2)], axis=0)
            sel = front[k, 0:1, :]
            both = jnp.concatenate([left * sel, left * (1.0 - sel)], axis=0)
            acc[:, 0:512] += jnp.dot(both, right, precision=HIGH, preferred_element_type=jnp.float32)
            acc[:, 512:640] += lax.dot_general(both, left, (((1,), (1,)), ((), ())), precision=HIGH, preferred_element_type=jnp.float32)

        return carry

    lax.fori_loop(0, PAIRS + LAG, step_fn, 0)

    give = pltpu.make_async_remote_copy(
        src_ref=acc.at[pl.ds(pl.multiple_of((1 - leaf) * 128, 128), 128)], dst_ref=part, send_sem=leaf_sem.at[0],
        recv_sem=leaf_sem.at[1], device_id=partner, device_id_type=MESH)
    give.start()
    give.wait_recv()
    own = pl.ds(pl.multiple_of(leaf * 128, 128), 128)
    acc[own] = acc[own] + part[...]

    def piece(j):
        return pl.ds(pl.multiple_of(leaf * 128 + j * 8, 8), 8)

    scat = []
    for j in range(1, 16):
        cp = pltpu.make_async_remote_copy(
            src_ref=acc.at[piece(lax.rem(row + j, rows_n))], dst_ref=full.at[1, pl.ds(j * 8, 8)], send_sem=rs_sem.at[0, j],
            recv_sem=rs_sem.at[1, j], device_id=peer(j), device_id_type=MESH)
        cp.start()
        scat.append(cp)
    total = acc[piece(row)]
    for j, cp in enumerate(scat):
        cp.wait_recv()
        total = total + full[1, pl.ds((j + 1) * 8, 8)]
    slot = pl.ds(pl.multiple_of(row * 8, 8), 8)
    full[0, slot] = total
    spread = []
    for j in range(1, 16):
        cp = pltpu.make_async_remote_copy(
            src_ref=full.at[0, slot], dst_ref=full.at[0, slot], send_sem=ag_sem.at[0, j],
            recv_sem=ag_sem.at[1, j], device_id=peer(j), device_id_type=MESH)
        cp.start()
        spread.append(cp)
    for cp in spread:
        cp.wait_recv()
    out[...] = full[0]

    give.wait_send()
    for cp in scat + spread:
        cp.wait_send()

    def finish(i, carry):
        for d in range(2):
            forward(i, d, drain)
            forward_other(i, d, drain)
        return carry

    lax.fori_loop(0, PAIRS, finish, 0)


def inverse_lower(d):
    n = d.shape[0]
    lane = lax.broadcasted_iota(jnp.int32, (n, 128), 1)
    line = lax.broadcasted_iota(jnp.int32, (n, 128), 0)
    cols = [jnp.broadcast_to(d[:, k:k + 1], (n, 128)) for k in range(n)]
    x = (lane == line).astype(jnp.float32)
    pivots = jnp.ones((n, 128), jnp.float32)
    for j in range(n):
        pivot = cols[j][j:j + 1, :]
        m = jnp.where(line > j, cols[j] * (1.0 / pivot), 0.0)
        for k in range(j + 1, n):
            cols[k] = cols[k] - m * cols[k][j:j + 1, :]
        x = x - m * x[j:j + 1, :]
        pivots = jnp.where(line == j, pivot, pivots)
    return (x / jnp.sqrt(pivots))[:, 0:n]


def solve_kernel(sums, out):
    col = lax.axis_index("col")
    n = 32
    rest = sums[...]
    done = []
    for b in range(4):
        at = 512 + b * n
        low = inverse_lower(rest[0:n, at:at + n])
        lead = jnp.dot(low, rest[0:n], precision=HIGH, preferred_element_type=jnp.float32)
        done.append(lead[:, 0:512])
        if b < 3:
            left = lead[:, at + n:640]
            rest = rest[n:] - lax.dot_general(left, lead, (((0,), (0,)), ((), ())), precision=HIGH, preferred_element_type=jnp.float32)
    top = jnp.concatenate(done, axis=0)
    place = (lax.broadcasted_iota(jnp.int32, (128, 512), 1) // EDGE) * 8 + col
    line = lax.broadcasted_iota(jnp.int32, (128, 512), 0) // EDGE
    out[0] = jnp.where(place >= line, top, 0.0)


def per_device(tiles, mask, dest):
    vmem = pl.BlockSpec(memory_space=pltpu.VMEM)
    dma = pltpu.SemaphoreType.DMA
    sums = pl.pallas_call(
        gather_kernel,
        out_shape=jax.ShapeDtypeStruct((128, 640), jnp.float32),
        in_specs=[pl.BlockSpec(memory_space=pl.ANY), vmem, vmem],
        out_specs=vmem,
        scratch_shapes=[
            pltpu.VMEM((32, 64, 512), jnp.float32),
            pltpu.VMEM((2, 16, 64, 128), jnp.float32),
            pltpu.VMEM((256, 640), jnp.float32),
            pltpu.VMEM((32, 8, 512), jnp.float32),
            pltpu.VMEM((PAIRS, 8, 256), jnp.float32),
            pltpu.VMEM((128, 640), jnp.float32),
            pltpu.VMEM((2, 128, 640), jnp.float32),
            dma((4,)), dma((2, 2, 16)), dma((2, 16)), dma((2,)), dma((2, 16)), dma((2, 16)),
        ],
        compiler_params=pltpu.CompilerParams(collective_id=0, has_side_effects=True),
    )(tiles, mask, dest)
    return pl.pallas_call(
        solve_kernel,
        out_shape=jax.ShapeDtypeStruct((1, 128, 512), jnp.float32),
        in_specs=[vmem],
        out_specs=vmem,
    )(sums)


def solution(mesh):
    in_specs = (
        P(("leaf", "row"), None, "col"),
        P(("leaf", "row"), "col"),
        P(("leaf", "row"), None),
    )
    return jax.shard_map(
        per_device, mesh=mesh, in_specs=in_specs, out_specs=P("leaf", None, "col"), check_vma=False
    )
```

```python
import functools

import jax
import jax.numpy as jnp
from jax import lax
from jax.experimental import pallas as pl
from jax.experimental.pallas import tpu as pltpu
from jax.sharding import PartitionSpec as P

MESH = pl.DeviceIdType.MESH
HIGH = lax.Precision.HIGHEST
EDGE = 64
PAIRS = 8
CHUNKS = 16
LAG = 6


def gather_kernel(tiles, mask, dest, out, wide, pan, acc, got, front, part, full, load_sem, send_sem, recv_sem, leaf_sem, rs_sem, ag_sem):
    leaf = lax.axis_index("leaf")
    row = lax.axis_index("row")
    col = lax.axis_index("col")
    y = col // 2
    mine = col % 2
    other = 1 - mine
    rows_n = lax.axis_size("row")

    def at(y_to, x_to):
        return (leaf, row, lax.rem(y_to + 4, 4) * 2 + x_to)

    up, down, across = at(y + 1, mine), at(y - 1, mine), at(y, other)
    middle = at(2, mine)
    peer = lambda j: (leaf, lax.rem(row + j, rows_n), col)
    partner = (1 - leaf, row, col)

    lanes = 128
    loads = []
    for b in range(4):
        span = pl.ds(b * lanes, lanes)
        loads.append(pltpu.make_async_copy(tiles.at[:, :, span], wide.at[:, :, span], load_sem.at[b]))
        loads[-1].start()

    barrier = pltpu.get_barrier_semaphore()
    targets = [up, down, across, partner] + [peer(j) for j in range(1, 16)]
    for t in targets:
        pl.semaphore_signal(barrier, inc=1, device_id=t, device_id_type=MESH)

    def blocks_of(rows_, width):
        shape = (rows_, width)
        return (lax.broadcasted_iota(jnp.int32, shape, 1) // EDGE == lax.broadcasted_iota(jnp.int32, shape, 0)).astype(jnp.float32)

    maskw = lax.dot_general(mask[...].astype(jnp.float32), blocks_of(8, 512), (((0,), (0,)), ((), ())), preferred_element_type=jnp.float32)
    in_first = jnp.broadcast_to((dest[...] < 16).astype(jnp.float32), (8, 32))
    first = jnp.dot(in_first, blocks_of(32, 2048), preferred_element_type=jnp.float32)
    for k in range(PAIRS):
        front[k] = first[:, k * 256:(k + 1) * 256]
    for t in range(32):
        got[t] = jnp.broadcast_to(maskw[t:t + 1], (8, 512))

    def copy_of(p, c, way, to):
        return pltpu.make_async_remote_copy(
            src_ref=pan.at[p, c], dst_ref=pan.at[p, c], send_sem=send_sem.at[way, p, c],
            recv_sem=recv_sem.at[p, c], device_id=to, device_id_type=MESH)

    edge_y = y == 0
    relay_y = lax.rem(y, 2) == 1

    def sends(c, act):
        half = jnp.logical_and(relay_y, lax.rem(c, 2) == y // 2)

        @pl.when(jnp.logical_or(edge_y, relay_y))
        def _():
            act(copy_of(mine, c, 0, across))

        @pl.when(edge_y)
        def _():
            act(copy_of(mine, c, 1, up))
            act(copy_of(mine, c, 2, down))

        @pl.when(half)
        def _():
            act(copy_of(mine, c, 1, middle))

    def sends_other(c, act):
        @pl.when(jnp.logical_and(relay_y, lax.rem(c, 2) == y // 2))
        def _():
            act(copy_of(other, c, 0, middle))

    start = lambda cp: cp.start()
    drain = lambda cp: cp.wait_send()

    loads[0].wait()
    pl.semaphore_wait(barrier, len(targets))

    @pl.when(y == 0)
    def _():
        def pack(c, carry):
            two = [wide[2 * c + t, :, 0:lanes] * got[2 * c + t, 0:1, 0:lanes] for t in range(2)]
            pan[mine, c] = jnp.concatenate(two, axis=0).T[0:EDGE, :]
            sends(c, start)
            return carry

        lax.fori_loop(0, CHUNKS, pack, 0)

    acc[...] = jnp.zeros_like(acc)
    for b in range(1, 4):
        loads[b].wait()

    def step_fn(i, carry):
        @pl.when(jnp.logical_and(i < CHUNKS, relay_y))
        def _():
            copy_of(mine, i, 0, up).wait_recv()
            sends(i, start)

        @pl.when(i >= LAG)
        def _():
            c = i - LAG

            @pl.when(y == 2)
            def _():
                copy_of(mine, c, 0, up).wait_recv()

            copy_of(other, c, 0, up).wait_recv()
            sends_other(c, start)

        @pl.when(jnp.logical_and(i >= LAG, lax.rem(i - LAG, 2) == 1))
        def _():
            k = (i - LAG) // 2
            right = []
            for t in range(4):
                tile = 4 * k + t
                right.append(wide[tile] * got[tile, 0:1, :])
            right = jnp.concatenate(right, axis=0)
            left = jnp.concatenate(
                [jnp.concatenate([pan[p, 2 * k], pan[p, 2 * k + 1]], axis=1) for p in range(2)], axis=0)
            sel = front[k, 0:1, :]
            both = jnp.concatenate([left * sel, left * (1.0 - sel)], axis=0)
            acc[:, 0:512] += jnp.dot(both, right, precision=HIGH, preferred_element_type=jnp.float32)
            acc[:, 512:640] += lax.dot_general(both, left, (((1,), (1,)), ((), ())), precision=HIGH, preferred_element_type=jnp.float32)

        return carry

    lax.fori_loop(0, CHUNKS + LAG, step_fn, 0)

    give = pltpu.make_async_remote_copy(
        src_ref=acc.at[pl.ds(pl.multiple_of((1 - leaf) * 128, 128), 128)], dst_ref=part, send_sem=leaf_sem.at[0],
        recv_sem=leaf_sem.at[1], device_id=partner, device_id_type=MESH)
    give.start()
    give.wait_recv()
    own = pl.ds(pl.multiple_of(leaf * 128, 128), 128)
    acc[own] = acc[own] + part[...]

    def piece(j):
        return pl.ds(pl.multiple_of(leaf * 128 + j * 8, 8), 8)

    scat = []
    for j in range(1, 16):
        cp = pltpu.make_async_remote_copy(
            src_ref=acc.at[piece(lax.rem(row + j, rows_n))], dst_ref=full.at[1, pl.ds(j * 8, 8)], send_sem=rs_sem.at[0, j],
            recv_sem=rs_sem.at[1, j], device_id=peer(j), device_id_type=MESH)
        cp.start()
        scat.append(cp)
    total = acc[piece(row)]
    for j, cp in enumerate(scat):
        cp.wait_recv()
        total = total + full[1, pl.ds((j + 1) * 8, 8)]
    slot = pl.ds(pl.multiple_of(row * 8, 8), 8)
    full[0, slot] = total
    spread = []
    for j in range(1, 16):
        cp = pltpu.make_async_remote_copy(
            src_ref=full.at[0, slot], dst_ref=full.at[0, slot], send_sem=ag_sem.at[0, j],
            recv_sem=ag_sem.at[1, j], device_id=peer(j), device_id_type=MESH)
        cp.start()
        spread.append(cp)
    for cp in spread:
        cp.wait_recv()
    out[...] = full[0]

    give.wait_send()
    for cp in scat + spread:
        cp.wait_send()

    def finish(c, carry):
        sends(c, drain)
        sends_other(c, drain)
        return carry

    lax.fori_loop(0, CHUNKS, finish, 0)


def inverse_lower(d):
    n = d.shape[0]
    lane = lax.broadcasted_iota(jnp.int32, (n, 128), 1)
    line = lax.broadcasted_iota(jnp.int32, (n, 128), 0)
    cols = [jnp.broadcast_to(d[:, k:k + 1], (n, 128)) for k in range(n)]
    x = (lane == line).astype(jnp.float32)
    pivots = jnp.ones((n, 128), jnp.float32)
    for j in range(n):
        pivot = cols[j][j:j + 1, :]
        m = jnp.where(line > j, cols[j] * (1.0 / pivot), 0.0)
        for k in range(j + 1, n):
            cols[k] = cols[k] - m * cols[k][j:j + 1, :]
        x = x - m * x[j:j + 1, :]
        pivots = jnp.where(line == j, pivot, pivots)
    return (x / jnp.sqrt(pivots))[:, 0:n]


def solve_kernel(sums, out):
    col = lax.axis_index("col")
    n = 32
    rest = sums[...]
    done = []
    for b in range(4):
        at = 512 + b * n
        low = inverse_lower(rest[0:n, at:at + n])
        lead = jnp.dot(low, rest[0:n], precision=HIGH, preferred_element_type=jnp.float32)
        done.append(lead[:, 0:512])
        if b < 3:
            left = lead[:, at + n:640]
            rest = rest[n:] - lax.dot_general(left, lead, (((0,), (0,)), ((), ())), precision=HIGH, preferred_element_type=jnp.float32)
    top = jnp.concatenate(done, axis=0)
    place = (lax.broadcasted_iota(jnp.int32, (128, 512), 1) // EDGE) * 8 + col
    line = lax.broadcasted_iota(jnp.int32, (128, 512), 0) // EDGE
    out[0] = jnp.where(place >= line, top, 0.0)


def per_device(tiles, mask, dest):
    vmem = pl.BlockSpec(memory_space=pltpu.VMEM)
    dma = pltpu.SemaphoreType.DMA
    sums = pl.pallas_call(
        gather_kernel,
        out_shape=jax.ShapeDtypeStruct((128, 640), jnp.float32),
        in_specs=[pl.BlockSpec(memory_space=pl.ANY), vmem, vmem],
        out_specs=vmem,
        scratch_shapes=[
            pltpu.VMEM((32, 64, 512), jnp.float32),
            pltpu.VMEM((2, 16, 64, 128), jnp.float32),
            pltpu.VMEM((256, 640), jnp.float32),
            pltpu.VMEM((32, 8, 512), jnp.float32),
            pltpu.VMEM((PAIRS, 8, 256), jnp.float32),
            pltpu.VMEM((128, 640), jnp.float32),
            pltpu.VMEM((2, 128, 640), jnp.float32),
            dma((4,)), dma((3, 2, CHUNKS)), dma((2, CHUNKS)), dma((2,)), dma((2, 16)), dma((2, 16)),
        ],
        compiler_params=pltpu.CompilerParams(collective_id=0, has_side_effects=True),
    )(tiles, mask.T, dest.T)
    return pl.pallas_call(
        solve_kernel,
        out_shape=jax.ShapeDtypeStruct((1, 128, 512), jnp.float32),
        in_specs=[vmem],
        out_specs=vmem,
    )(sums)


def solution(mesh):
    in_specs = (
        P(("leaf", "row"), None, "col"),
        P(("leaf", "row"), "col"),
        P(("leaf", "row"), None),
    )
    return jax.shard_map(
        per_device, mesh=mesh, in_specs=in_specs, out_specs=P("leaf", None, "col"), check_vma=False
    )
```

```python
import functools

import jax
import jax.numpy as jnp
from jax import lax
from jax.experimental import pallas as pl
from jax.experimental.pallas import tpu as pltpu
from jax.sharding import PartitionSpec as P

MESH = pl.DeviceIdType.MESH
HIGH = lax.Precision.HIGHEST
EDGE = 64
PAIRS = 8
CHUNKS = 16
LAG = 6
FAR_FIRST = (8, 7, 9, 6, 10, 5, 11, 4, 12, 3, 13, 2, 14, 1, 15)


def gather_kernel(tiles, mask, dest, out, wide, pan, acc, gram, got, front, part, part_g, come, come_g, full, full_g, load_sem, send_sem, recv_sem, leaf_sem, rs_sem, ag_sem):
    leaf = lax.axis_index("leaf")
    row = lax.axis_index("row")
    col = lax.axis_index("col")
    y = col // 2
    mine = col % 2
    other = 1 - mine
    rows_n = lax.axis_size("row")

    def at(y_to, x_to):
        return (leaf, row, lax.rem(y_to + 4, 4) * 2 + x_to)

    up, down, across = at(y + 1, mine), at(y - 1, mine), at(y, other)
    middle = at(2, mine)
    peer = lambda j: (leaf, lax.rem(row + j, rows_n), col)
    partner = (1 - leaf, row, col)

    lanes = 128
    loads = []
    for b in range(4):
        span = pl.ds(b * lanes, lanes)
        loads.append(pltpu.make_async_copy(tiles.at[:, :, span], wide.at[:, :, span], load_sem.at[b]))
    loads[0].start()

    barrier = pltpu.get_barrier_semaphore()
    targets = [up, down, across, partner] + [peer(j) for j in range(1, 16)]
    for t in targets:
        pl.semaphore_signal(barrier, inc=1, device_id=t, device_id_type=MESH)

    def blocks_of(rows_, width):
        shape = (rows_, width)
        return (lax.broadcasted_iota(jnp.int32, shape, 1) // EDGE == lax.broadcasted_iota(jnp.int32, shape, 0)).astype(jnp.float32)

    maskw = lax.dot_general(mask[...].astype(jnp.float32), blocks_of(8, 512), (((0,), (0,)), ((), ())), preferred_element_type=jnp.float32)
    in_first = jnp.broadcast_to((dest[...] < 16).astype(jnp.float32), (8, 32))
    first = jnp.dot(in_first, blocks_of(32, 2048), preferred_element_type=jnp.float32)
    for k in range(PAIRS):
        front[k] = first[:, k * 256:(k + 1) * 256]
    for t in range(32):
        got[t] = jnp.broadcast_to(maskw[t:t + 1], (8, 512))

    def copy_of(p, c, way, to):
        return pltpu.make_async_remote_copy(
            src_ref=pan.at[p, c], dst_ref=pan.at[p, c], send_sem=send_sem.at[way, p, c],
            recv_sem=recv_sem.at[p, c], device_id=to, device_id_type=MESH)

    edge_y = y == 0
    relay_y = lax.rem(y, 2) == 1

    def sends(c, act):
        half = jnp.logical_and(relay_y, lax.rem(c, 2) == y // 2)

        @pl.when(jnp.logical_or(edge_y, relay_y))
        def _():
            act(copy_of(mine, c, 0, across))

        @pl.when(edge_y)
        def _():
            act(copy_of(mine, c, 1, up))
            act(copy_of(mine, c, 2, down))

        @pl.when(half)
        def _():
            act(copy_of(mine, c, 1, middle))

    def sends_other(c, act):
        @pl.when(jnp.logical_and(relay_y, lax.rem(c, 2) == y // 2))
        def _():
            act(copy_of(other, c, 0, middle))

    for b in range(1, 4):
        loads[b].start()
    start = lambda cp: cp.start()
    drain = lambda cp: cp.wait_send()

    loads[0].wait()
    pl.semaphore_wait(barrier, len(targets))

    @pl.when(y == 0)
    def _():
        def pack(c, carry):
            two = [wide[2 * c + t, :, 0:lanes] * got[2 * c + t, 0:1, 0:lanes] for t in range(2)]
            pan[mine, c] = jnp.concatenate(two, axis=0).T[0:EDGE, :]
            sends(c, start)
            return carry

        lax.fori_loop(0, CHUNKS, pack, 0)

    acc[...] = jnp.zeros_like(acc)
    gram[...] = jnp.zeros_like(gram)
    for b in range(1, 4):
        loads[b].wait()

    def step_fn(i, carry):
        @pl.when(jnp.logical_and(i < CHUNKS, relay_y))
        def _():
            copy_of(mine, i, 0, up).wait_recv()
            sends(i, start)

        @pl.when(i >= LAG)
        def _():
            c = i - LAG

            @pl.when(y == 2)
            def _():
                copy_of(mine, c, 0, up).wait_recv()

            copy_of(other, c, 0, up).wait_recv()
            sends_other(c, start)

        @pl.when(jnp.logical_and(i >= LAG, lax.rem(i - LAG, 2) == 1))
        def _():
            k = (i - LAG) // 2
            right = []
            for t in range(4):
                tile = 4 * k + t
                right.append(wide[tile] * got[tile, 0:1, :])
            right = jnp.concatenate(right, axis=0)
            left = jnp.concatenate(
                [jnp.concatenate([pan[p, 2 * k], pan[p, 2 * k + 1]], axis=1) for p in range(2)], axis=0)
            sel = front[k, 0:1, :]
            both = jnp.concatenate([left * sel, left * (1.0 - sel)], axis=0)
            gram[...] += lax.dot_general(both, left, (((1,), (1,)), ((), ())), precision=HIGH, preferred_element_type=jnp.float32)
            for h in range(2):
                acc[h] += jnp.dot(both, right[:, h * 256:(h + 1) * 256], precision=HIGH, preferred_element_type=jnp.float32)

        return carry

    lax.fori_loop(0, CHUNKS + LAG, step_fn, 0)

    other_rows = pl.ds(pl.multiple_of((1 - leaf) * 128, 128), 128)
    own_rows = pl.ds(pl.multiple_of(leaf * 128, 128), 128)
    slot = pl.ds(pl.multiple_of(row * 8, 8), 8)

    def remote(src, dst, sems, n, to):
        cp = pltpu.make_async_remote_copy(
            src_ref=src, dst_ref=dst, send_sem=sems.at[(0,) + n], recv_sem=sems.at[(1,) + n], device_id=to, device_id_type=MESH)
        cp.start()
        return cp

    sums = [gram, acc.at[0], acc.at[1]]
    parts = [part_g, part.at[0], part.at[1]]
    comes = [come_g, come.at[0], come.at[1]]
    fulls = [full_g, full.at[0], full.at[1]]
    gives = [remote(sums[t].at[other_rows], parts[t], leaf_sem, (t,), partner) for t in range(3)]
    sent = list(gives)

    def piece(j):
        return pl.ds(pl.multiple_of(leaf * 128 + lax.rem(row + j, rows_n) * 8, 8), 8)

    scats = []
    for t in range(3):
        gives[t].wait_recv()
        sums[t][own_rows] = sums[t][own_rows] + parts[t][...]
        scats.append([remote(sums[t].at[piece(j)], comes[t].at[j], rs_sem, (t, j), peer(j)) for j in FAR_FIRST])
        sent += scats[t]
    spreads = []
    for t in range(3):
        for cp in scats[t]:
            cp.wait_recv()
        total = sums[t][piece(0)]
        for j in range(1, 16):
            total = total + comes[t][j]
        fulls[t][slot] = total
        spreads.append([remote(fulls[t].at[slot], fulls[t].at[slot], ag_sem, (t, j), peer(j)) for j in FAR_FIRST])
        sent += spreads[t]

    for cp in spreads[0]:
        cp.wait_recv()
    low = inverse_of_factor(full_g[...])
    line = lax.broadcasted_iota(jnp.int32, (128, 256), 0) // EDGE
    for h in range(2):
        for cp in spreads[1 + h]:
            cp.wait_recv()
        top = jnp.dot(low, full[h], precision=HIGH, preferred_element_type=jnp.float32)
        place = (lax.broadcasted_iota(jnp.int32, (128, 256), 1) // EDGE + 4 * h) * 8 + col
        out[0, :, h * 256:(h + 1) * 256] = jnp.where(place >= line, top, 0.0)

    for cp in sent:
        cp.wait_send()

    def finish(c, carry):
        sends(c, drain)
        sends_other(c, drain)
        return carry

    lax.fori_loop(0, CHUNKS, finish, 0)


def inverse_lower(d):
    n = d.shape[0]
    lane = lax.broadcasted_iota(jnp.int32, (n, 128), 1)
    line = lax.broadcasted_iota(jnp.int32, (n, 128), 0)
    cols = [jnp.broadcast_to(d[:, k:k + 1], (n, 128)) for k in range(n)]
    x = (lane == line).astype(jnp.float32)
    pivots = jnp.ones((n, 128), jnp.float32)
    for j in range(n):
        pivot = cols[j][j:j + 1, :]
        m = jnp.where(line > j, cols[j] * (1.0 / pivot), 0.0)
        for k in range(j + 1, n):
            cols[k] = cols[k] - m * cols[k][j:j + 1, :]
        x = x - m * x[j:j + 1, :]
        pivots = jnp.where(line == j, pivot, pivots)
    return (x / jnp.sqrt(pivots))[:, 0:n]


def inverse_of_factor(g):
    n = 32
    size = g.shape[0]
    eye = (lax.broadcasted_iota(jnp.int32, g.shape, 0) == lax.broadcasted_iota(jnp.int32, g.shape, 1)).astype(jnp.float32)
    rest = jnp.concatenate([eye, g], axis=1)
    done = []
    for b in range(size // n):
        at = size + b * n
        low = inverse_lower(rest[0:n, at:at + n])
        lead = jnp.dot(low, rest[0:n], precision=HIGH, preferred_element_type=jnp.float32)
        done.append(lead[:, 0:size])
        if b + 1 < size // n:
            left = lead[:, at + n:2 * size]
            rest = rest[n:] - lax.dot_general(left, lead, (((0,), (0,)), ((), ())), precision=HIGH, preferred_element_type=jnp.float32)
    return jnp.concatenate(done, axis=0)


def per_device(tiles, mask, dest):
    vmem = pl.BlockSpec(memory_space=pltpu.VMEM)
    dma = pltpu.SemaphoreType.DMA
    return pl.pallas_call(
        gather_kernel,
        out_shape=jax.ShapeDtypeStruct((1, 128, 512), jnp.float32),
        in_specs=[pl.BlockSpec(memory_space=pl.ANY), vmem, vmem],
        out_specs=vmem,
        scratch_shapes=[
            pltpu.VMEM((32, 64, 512), jnp.float32),
            pltpu.VMEM((2, CHUNKS, 64, 128), jnp.float32),
            pltpu.VMEM((2, 256, 256), jnp.float32),
            pltpu.VMEM((256, 128), jnp.float32),
            pltpu.VMEM((32, 8, 512), jnp.float32),
            pltpu.VMEM((PAIRS, 8, 256), jnp.float32),
            pltpu.VMEM((2, 128, 256), jnp.float32),
            pltpu.VMEM((128, 128), jnp.float32),
            pltpu.VMEM((2, 16, 8, 256), jnp.float32),
            pltpu.VMEM((16, 8, 128), jnp.float32),
            pltpu.VMEM((2, 128, 256), jnp.float32),
            pltpu.VMEM((128, 128), jnp.float32),
            dma((4,)), dma((3, 2, CHUNKS)), dma((2, CHUNKS)), dma((2, 3)), dma((2, 3, 16)), dma((2, 3, 16)),
        ],
        compiler_params=pltpu.CompilerParams(collective_id=0, has_side_effects=True),
    )(tiles, mask.T, dest.T)


def solution(mesh):
    in_specs = (
        P(("leaf", "row"), None, "col"),
        P(("leaf", "row"), "col"),
        P(("leaf", "row"), None),
    )
    return jax.shard_map(
        per_device, mesh=mesh, in_specs=in_specs, out_specs=P("leaf", None, "col"), check_vma=False
    )
```

```python
import functools

import jax
import jax.numpy as jnp
from jax import lax
from jax.experimental import pallas as pl
from jax.experimental.pallas import tpu as pltpu
from jax.sharding import PartitionSpec as P

MESH = pl.DeviceIdType.MESH
HIGH = lax.Precision.HIGHEST
EDGE = 64
PAIRS = 8
CHUNKS = 16
LAG = 6
FAR_FIRST = (8, 7, 9, 6, 10, 5, 11, 4, 12, 3, 13, 2, 14, 1, 15)


def split_dot(a, b):
    a_high, b_high = a.astype(jnp.bfloat16), b.astype(jnp.bfloat16)
    a_low = (a - a_high.astype(jnp.float32)).astype(jnp.bfloat16)
    b_low = (b - b_high.astype(jnp.float32)).astype(jnp.bfloat16)
    dot = functools.partial(jnp.dot, preferred_element_type=jnp.float32)
    return dot(a_high, b_high) + (dot(a_low, b_high) + dot(a_high, b_low))


def gather_kernel(tiles, mask_in, dest_in, out, mask, dest, wide, pan, acc, gram, got, front, part, part_g, come, come_g, full, full_g, load_sem, send_sem, recv_sem, leaf_sem, rs_sem, ag_sem):
    leaf = lax.axis_index("leaf")
    row = lax.axis_index("row")
    col = lax.axis_index("col")
    y = col // 2
    mine = col % 2
    other = 1 - mine
    rows_n = lax.axis_size("row")

    def at(y_to, x_to):
        return (leaf, row, lax.rem(y_to + 4, 4) * 2 + x_to)

    up, down, across = at(y + 1, mine), at(y - 1, mine), at(y, other)
    middle = at(2, mine)
    peer = lambda j: (leaf, lax.rem(row + j, rows_n), col)
    partner = (1 - leaf, row, col)

    lanes = 128
    loads = []
    for b in range(4):
        span = pl.ds(b * lanes, lanes)
        loads.append(pltpu.make_async_copy(tiles.at[:, :, span], wide.at[:, :, span], load_sem.at[b]))
    loads[0].start()

    small = [pltpu.make_async_copy(mask_in, mask, load_sem.at[4]), pltpu.make_async_copy(dest_in, dest, load_sem.at[5])]
    for cp in small:
        cp.start()

    barrier = pltpu.get_barrier_semaphore()
    targets = [up, down, across, partner] + [peer(j) for j in range(1, 16)]
    for t in targets:
        pl.semaphore_signal(barrier, inc=1, device_id=t, device_id_type=MESH)

    def blocks_of(rows_, width):
        shape = (rows_, width)
        return (lax.broadcasted_iota(jnp.int32, shape, 1) // EDGE == lax.broadcasted_iota(jnp.int32, shape, 0)).astype(jnp.float32)

    for cp in small:
        cp.wait()
    maskw = lax.dot_general(mask[...].astype(jnp.float32), blocks_of(8, 512), (((0,), (0,)), ((), ())), preferred_element_type=jnp.float32)
    in_first = jnp.broadcast_to((dest[...] < 16).astype(jnp.float32), (8, 32))
    first = jnp.dot(in_first, blocks_of(32, 2048), preferred_element_type=jnp.float32)
    for k in range(PAIRS):
        front[k] = first[:, k * 256:(k + 1) * 256]
    for t in range(32):
        got[t] = jnp.broadcast_to(maskw[t:t + 1], (8, 512))

    def copy_of(p, c, way, to):
        return pltpu.make_async_remote_copy(
            src_ref=pan.at[p, c], dst_ref=pan.at[p, c], send_sem=send_sem.at[way, p, c],
            recv_sem=recv_sem.at[p, c], device_id=to, device_id_type=MESH)

    edge_y = y == 0
    relay_y = lax.rem(y, 2) == 1

    def sends(c, act):
        half = jnp.logical_and(relay_y, lax.rem(c, 2) == y // 2)

        @pl.when(jnp.logical_or(edge_y, relay_y))
        def _():
            act(copy_of(mine, c, 0, across))

        @pl.when(edge_y)
        def _():
            act(copy_of(mine, c, 1, up))
            act(copy_of(mine, c, 2, down))

        @pl.when(half)
        def _():
            act(copy_of(mine, c, 1, middle))

    def sends_other(c, act):
        @pl.when(jnp.logical_and(relay_y, lax.rem(c, 2) == y // 2))
        def _():
            act(copy_of(other, c, 0, middle))

    for b in range(1, 4):
        loads[b].start()
    start = lambda cp: cp.start()
    drain = lambda cp: cp.wait_send()

    loads[0].wait()
    pl.semaphore_wait(barrier, len(targets))

    @pl.when(y == 0)
    def _():
        def pack(c, carry):
            two = [wide[2 * c + t, :, 0:lanes] * got[2 * c + t, 0:1, 0:lanes] for t in range(2)]
            pan[mine, c] = jnp.concatenate(two, axis=0).T[0:EDGE, :]
            sends(c, start)
            return carry

        lax.fori_loop(0, CHUNKS, pack, 0)

    acc[...] = jnp.zeros_like(acc)
    gram[...] = jnp.zeros_like(gram)
    for b in range(1, 4):
        loads[b].wait()

    def step_fn(i, carry):
        @pl.when(jnp.logical_and(i < CHUNKS, relay_y))
        def _():
            copy_of(mine, i, 0, up).wait_recv()
            sends(i, start)

        @pl.when(i >= LAG)
        def _():
            c = i - LAG

            @pl.when(y == 2)
            def _():
                copy_of(mine, c, 0, up).wait_recv()

            copy_of(other, c, 0, up).wait_recv()
            sends_other(c, start)

        @pl.when(jnp.logical_and(i >= LAG, lax.rem(i - LAG, 2) == 1))
        def _():
            k = (i - LAG) // 2
            right = []
            for t in range(4):
                tile = 4 * k + t
                right.append(wide[tile] * got[tile, 0:1, :])
            right = jnp.concatenate(right, axis=0)
            left = jnp.concatenate(
                [jnp.concatenate([pan[p, 2 * k], pan[p, 2 * k + 1]], axis=1) for p in range(2)], axis=0)
            sel = front[k, 0:1, :]
            both = jnp.concatenate([left * sel, left * (1.0 - sel)], axis=0)
            gram[...] += lax.dot_general(both, left, (((1,), (1,)), ((), ())), precision=HIGH, preferred_element_type=jnp.float32)
            acc[...] += split_dot(both, right)

        return carry

    lax.fori_loop(0, CHUNKS + LAG, step_fn, 0)

    other_rows = pl.ds(pl.multiple_of((1 - leaf) * 128, 128), 128)
    own_rows = pl.ds(pl.multiple_of(leaf * 128, 128), 128)
    slot = pl.ds(pl.multiple_of(row * 8, 8), 8)

    def remote(src, dst, sems, n, to):
        cp = pltpu.make_async_remote_copy(
            src_ref=src, dst_ref=dst, send_sem=sems.at[(0,) + n], recv_sem=sems.at[(1,) + n], device_id=to, device_id_type=MESH)
        cp.start()
        return cp

    sums = [gram, acc]
    parts = [part_g, part]
    comes = [come_g, come]
    fulls = [full_g, full]
    gives = [remote(sums[t].at[other_rows], parts[t], leaf_sem, (t,), partner) for t in range(2)]
    sent = list(gives)

    def piece(j):
        return pl.ds(pl.multiple_of(leaf * 128 + lax.rem(row + j, rows_n) * 8, 8), 8)

    scats = []
    for t in range(2):
        gives[t].wait_recv()
        sums[t][own_rows] = sums[t][own_rows] + parts[t][...]
        scats.append([remote(sums[t].at[piece(j)], comes[t].at[j], rs_sem, (t, j), peer(j)) for j in FAR_FIRST])
        sent += scats[t]
    spreads = []
    for t in range(2):
        for cp in scats[t]:
            cp.wait_recv()
        total = sums[t][piece(0)]
        for j in range(1, 16):
            total = total + comes[t][j]
        fulls[t][slot] = total
        spreads.append([remote(fulls[t].at[slot], fulls[t].at[slot], ag_sem, (t, j), peer(j)) for j in FAR_FIRST])
        sent += spreads[t]

    for cp in spreads[0]:
        cp.wait_recv()
    low = inverse_of_factor(full_g[...])
    line = lax.broadcasted_iota(jnp.int32, (128, 512), 0) // EDGE
    place = (lax.broadcasted_iota(jnp.int32, (128, 512), 1) // EDGE) * 8 + col
    for cp in spreads[1]:
        cp.wait_recv()
    top = jnp.dot(low, full[...], precision=HIGH, preferred_element_type=jnp.float32)
    out[0] = jnp.where(place >= line, top, 0.0)

    for cp in sent:
        cp.wait_send()

    def finish(c, carry):
        sends(c, drain)
        sends_other(c, drain)
        return carry

    lax.fori_loop(0, CHUNKS, finish, 0)


def inverse_lower(d):
    n = d.shape[0]
    lane = lax.broadcasted_iota(jnp.int32, (n, 128), 1)
    line = lax.broadcasted_iota(jnp.int32, (n, 128), 0)
    cols = [jnp.broadcast_to(d[:, k:k + 1], (n, 128)) for k in range(n)]
    x = (lane == line).astype(jnp.float32)
    pivots = jnp.ones((n, 128), jnp.float32)
    for j in range(n):
        pivot = cols[j][j:j + 1, :]
        m = jnp.where(line > j, cols[j] * (1.0 / pivot), 0.0)
        for k in range(j + 1, n):
            cols[k] = cols[k] - m * cols[k][j:j + 1, :]
        x = x - m * x[j:j + 1, :]
        pivots = jnp.where(line == j, pivot, pivots)
    return (x / jnp.sqrt(pivots))[:, 0:n]


def inverse_of_factor(g):
    n = 32
    size = g.shape[0]
    eye = (lax.broadcasted_iota(jnp.int32, g.shape, 0) == lax.broadcasted_iota(jnp.int32, g.shape, 1)).astype(jnp.float32)
    rest = jnp.concatenate([eye, g], axis=1)
    done = []
    for b in range(size // n):
        at = size + b * n
        low = inverse_lower(rest[0:n, at:at + n])
        lead = jnp.dot(low, rest[0:n], precision=HIGH, preferred_element_type=jnp.float32)
        done.append(lead[:, 0:size])
        if b + 1 < size // n:
            left = lead[:, at + n:2 * size]
            rest = rest[n:] - lax.dot_general(left, lead, (((0,), (0,)), ((), ())), precision=HIGH, preferred_element_type=jnp.float32)
    return jnp.concatenate(done, axis=0)


def per_device(tiles, mask, dest):
    vmem = pl.BlockSpec(memory_space=pltpu.VMEM)
    dma = pltpu.SemaphoreType.DMA
    return pl.pallas_call(
        gather_kernel,
        out_shape=jax.ShapeDtypeStruct((1, 128, 512), jnp.float32),
        in_specs=[pl.BlockSpec(memory_space=pl.ANY)] * 3,
        out_specs=vmem,
        scratch_shapes=[
            pltpu.VMEM((8, 32), jnp.int32),
            pltpu.VMEM((1, 32), jnp.int32),
            pltpu.VMEM((32, 64, 512), jnp.float32),
            pltpu.VMEM((2, CHUNKS, 64, 128), jnp.float32),
            pltpu.VMEM((256, 512), jnp.float32),
            pltpu.VMEM((256, 128), jnp.float32),
            pltpu.VMEM((32, 8, 512), jnp.float32),
            pltpu.VMEM((PAIRS, 8, 256), jnp.float32),
            pltpu.VMEM((128, 512), jnp.float32),
            pltpu.VMEM((128, 128), jnp.float32),
            pltpu.VMEM((16, 8, 512), jnp.float32),
            pltpu.VMEM((16, 8, 128), jnp.float32),
            pltpu.VMEM((128, 512), jnp.float32),
            pltpu.VMEM((128, 128), jnp.float32),
            dma((6,)), dma((3, 2, CHUNKS)), dma((2, CHUNKS)), dma((2, 2)), dma((2, 2, 16)), dma((2, 2, 16)),
        ],
        compiler_params=pltpu.CompilerParams(collective_id=0, has_side_effects=True),
    )(tiles, mask.T, dest.T)


def solution(mesh):
    in_specs = (
        P(("leaf", "row"), None, "col"),
        P(("leaf", "row"), "col"),
        P(("leaf", "row"), None),
    )
    return jax.shard_map(
        per_device, mesh=mesh, in_specs=in_specs, out_specs=P("leaf", None, "col"), check_vma=False
    )
```

```python
import functools

import jax
import jax.numpy as jnp
from jax import lax
from jax.experimental import pallas as pl
from jax.experimental.pallas import tpu as pltpu
from jax.sharding import PartitionSpec as P

MESH = pl.DeviceIdType.MESH
HIGH = lax.Precision.HIGHEST
EDGE = 64
PAIRS = 8
CHUNKS = 16
LAG = 8
FAR_FIRST = (8, 7, 9, 6, 10, 5, 11, 4, 12, 3, 13, 2, 14, 1, 15)


def split_dot(a, b):
    a_high, b_high = a.astype(jnp.bfloat16), b.astype(jnp.bfloat16)
    a_low = (a - a_high.astype(jnp.float32)).astype(jnp.bfloat16)
    b_low = (b - b_high.astype(jnp.float32)).astype(jnp.bfloat16)
    dot = functools.partial(jnp.dot, preferred_element_type=jnp.float32)
    return dot(a_high, b_high) + (dot(a_low, b_high) + dot(a_high, b_low))


def gather_kernel(tiles, mask_in, dest_in, out, mask, dest, wide, pan, acc, gram, got, front, part, part_g, come, come_g, full, full_g, load_sem, send_sem, recv_sem, leaf_sem, rs_sem, ag_sem):
    leaf = lax.axis_index("leaf")
    row = lax.axis_index("row")
    col = lax.axis_index("col")
    y = col // 2
    mine = col % 2
    other = 1 - mine
    rows_n = lax.axis_size("row")

    def at(y_to, x_to):
        return (leaf, row, lax.rem(y_to + 4, 4) * 2 + x_to)

    up, down, across = at(y + 1, mine), at(y - 1, mine), at(y, other)
    middle = at(2, mine)
    peer = lambda j: (leaf, lax.rem(row + j, rows_n), col)
    partner = (1 - leaf, row, col)

    lanes = 128
    loads = []
    for b in range(4):
        span = pl.ds(b * lanes, lanes)
        loads.append(pltpu.make_async_copy(tiles.at[:, :, span], wide.at[:, :, span], load_sem.at[b]))
    loads[0].start()

    small = [pltpu.make_async_copy(mask_in, mask, load_sem.at[4]), pltpu.make_async_copy(dest_in, dest, load_sem.at[5])]
    for cp in small:
        cp.start()

    barrier = pltpu.get_barrier_semaphore()
    targets = [up, down, across, partner] + [peer(j) for j in range(1, 16)]
    for t in targets:
        pl.semaphore_signal(barrier, inc=1, device_id=t, device_id_type=MESH)

    def blocks_of(rows_, width):
        shape = (rows_, width)
        return (lax.broadcasted_iota(jnp.int32, shape, 1) // EDGE == lax.broadcasted_iota(jnp.int32, shape, 0)).astype(jnp.float32)

    for cp in small:
        cp.wait()
    maskw = lax.dot_general(mask[...].astype(jnp.float32), blocks_of(8, 512), (((0,), (0,)), ((), ())), preferred_element_type=jnp.float32)
    in_first = jnp.broadcast_to((dest[...] < 16).astype(jnp.float32), (8, 32))
    first = jnp.dot(in_first, blocks_of(32, 2048), preferred_element_type=jnp.float32)
    for k in range(PAIRS):
        front[k] = first[:, k * 256:(k + 1) * 256]
    for t in range(32):
        got[t] = jnp.broadcast_to(maskw[t:t + 1], (8, 512))

    def copy_of(p, c, way, to):
        return pltpu.make_async_remote_copy(
            src_ref=pan.at[p, c], dst_ref=pan.at[p, c], send_sem=send_sem.at[way, p, c],
            recv_sem=recv_sem.at[p, c], device_id=to, device_id_type=MESH)

    edge_y = y == 0
    relay_y = lax.rem(y, 2) == 1

    def sends(c, act):
        half = jnp.logical_and(relay_y, lax.rem(c, 2) == y // 2)

        act(copy_of(mine, c, 0, across))

        @pl.when(edge_y)
        def _():
            act(copy_of(mine, c, 1, up))
            act(copy_of(mine, c, 2, down))

        @pl.when(half)
        def _():
            act(copy_of(mine, c, 1, middle))

    for b in range(1, 4):
        loads[b].start()
    start = lambda cp: cp.start()
    drain = lambda cp: cp.wait_send()

    loads[0].wait()
    pl.semaphore_wait(barrier, len(targets))

    @pl.when(y == 0)
    def _():
        def pack(c, carry):
            two = [wide[2 * c + t, :, 0:lanes] * got[2 * c + t, 0:1, 0:lanes] for t in range(2)]
            pan[mine, c] = jnp.concatenate(two, axis=0).T[0:EDGE, :]
            sends(c, start)
            return carry

        lax.fori_loop(0, CHUNKS, pack, 0)

    acc[...] = jnp.zeros_like(acc)
    gram[...] = jnp.zeros_like(gram)
    for b in range(1, 4):
        loads[b].wait()

    def step_fn(i, carry):
        @pl.when(jnp.logical_and(i < CHUNKS, y > 0))
        def _():
            copy_of(mine, i, 0, up).wait_recv()
            sends(i, start)

        @pl.when(i >= LAG)
        def _():
            c = i - LAG

            copy_of(other, c, 0, up).wait_recv()

        @pl.when(jnp.logical_and(i >= LAG, lax.rem(i - LAG, 2) == 1))
        def _():
            k = (i - LAG) // 2
            right = []
            for t in range(4):
                tile = 4 * k + t
                right.append(wide[tile] * got[tile, 0:1, :])
            right = jnp.concatenate(right, axis=0)
            left = jnp.concatenate(
                [jnp.concatenate([pan[p, 2 * k], pan[p, 2 * k + 1]], axis=1) for p in range(2)], axis=0)
            sel = front[k, 0:1, :]
            both = jnp.concatenate([left * sel, left * (1.0 - sel)], axis=0)
            gram[...] += lax.dot_general(both, left, (((1,), (1,)), ((), ())), precision=HIGH, preferred_element_type=jnp.float32)
            acc[...] += split_dot(both, right)

        return carry

    lax.fori_loop(0, CHUNKS + LAG, step_fn, 0)

    other_rows = pl.ds(pl.multiple_of((1 - leaf) * 128, 128), 128)
    own_rows = pl.ds(pl.multiple_of(leaf * 128, 128), 128)
    slot = pl.ds(pl.multiple_of(row * 8, 8), 8)

    def remote(src, dst, sems, n, to):
        cp = pltpu.make_async_remote_copy(
            src_ref=src, dst_ref=dst, send_sem=sems.at[(0,) + n], recv_sem=sems.at[(1,) + n], device_id=to, device_id_type=MESH)
        cp.start()
        return cp

    sums = [gram, acc]
    parts = [part_g, part]
    comes = [come_g, come]
    fulls = [full_g, full]
    gives = [remote(sums[t].at[other_rows], parts[t], leaf_sem, (t,), partner) for t in range(2)]

    def piece(j):
        return pl.ds(pl.multiple_of(leaf * 128 + lax.rem(row + j, rows_n) * 8, 8), 8)

    scats = []
    for t in range(2):
        gives[t].wait_recv()
        sums[t][own_rows] = sums[t][own_rows] + parts[t][...]
        scats.append([remote(sums[t].at[piece(j)], comes[t].at[j], rs_sem, (t, j), peer(j)) for j in FAR_FIRST])
    spreads = []
    for t in range(2):
        for cp in scats[t]:
            cp.wait_recv()
        total = sums[t][piece(0)]
        for j in range(1, 16):
            total = total + comes[t][j]
        fulls[t][slot] = total
        spreads.append([remote(fulls[t].at[slot], fulls[t].at[slot], ag_sem, (t, j), peer(j)) for j in FAR_FIRST])

    def finish(c, carry):
        sends(c, drain)
        return carry

    lax.fori_loop(0, CHUNKS, finish, 0)
    for cp in gives + scats[0] + scats[1]:
        cp.wait_send()
    for cp in spreads[0]:
        cp.wait_recv()
    low = inverse_of_factor(full_g[...])
    for cp in spreads[0]:
        cp.wait_send()
    line = lax.broadcasted_iota(jnp.int32, (128, 512), 0) // EDGE
    place = (lax.broadcasted_iota(jnp.int32, (128, 512), 1) // EDGE) * 8 + col
    for cp in spreads[1]:
        cp.wait_recv()
    top = jnp.dot(low, full[...], precision=HIGH, preferred_element_type=jnp.float32)
    out[0] = jnp.where(place >= line, top, 0.0)

    for cp in spreads[1]:
        cp.wait_send()


def inverse_lower(d):
    n = d.shape[0]
    lane = lax.broadcasted_iota(jnp.int32, (n, 128), 1)
    line = lax.broadcasted_iota(jnp.int32, (n, 128), 0)
    cols = [jnp.broadcast_to(d[:, k:k + 1], (n, 128)) for k in range(n)]
    x = (lane == line).astype(jnp.float32)
    pivots = jnp.ones((n, 128), jnp.float32)
    for j in range(n):
        pivot = cols[j][j:j + 1, :]
        m = jnp.where(line > j, cols[j] * (1.0 / pivot), 0.0)
        for k in range(j + 1, n):
            cols[k] = cols[k] - m * cols[k][j:j + 1, :]
        x = x - m * x[j:j + 1, :]
        pivots = jnp.where(line == j, pivot, pivots)
    return (x / jnp.sqrt(pivots))[:, 0:n]


def inverse_of_factor(g):
    n = 32
    size = g.shape[0]
    eye = (lax.broadcasted_iota(jnp.int32, g.shape, 0) == lax.broadcasted_iota(jnp.int32, g.shape, 1)).astype(jnp.float32)
    rest = jnp.concatenate([eye, g], axis=1)
    done = []
    for b in range(size // n):
        at = size + b * n
        low = inverse_lower(rest[0:n, at:at + n])
        lead = jnp.dot(low, rest[0:n], precision=HIGH, preferred_element_type=jnp.float32)
        done.append(lead[:, 0:size])
        if b + 1 < size // n:
            left = lead[:, at + n:2 * size]
            rest = rest[n:] - lax.dot_general(left, lead, (((0,), (0,)), ((), ())), precision=HIGH, preferred_element_type=jnp.float32)
    return jnp.concatenate(done, axis=0)


def per_device(tiles, mask, dest):
    vmem = pl.BlockSpec(memory_space=pltpu.VMEM)
    dma = pltpu.SemaphoreType.DMA
    return pl.pallas_call(
        gather_kernel,
        out_shape=jax.ShapeDtypeStruct((1, 128, 512), jnp.float32),
        in_specs=[pl.BlockSpec(memory_space=pl.ANY)] * 3,
        out_specs=vmem,
        scratch_shapes=[
            pltpu.VMEM((8, 32), jnp.int32),
            pltpu.VMEM((1, 32), jnp.int32),
            pltpu.VMEM((32, 64, 512), jnp.float32),
            pltpu.VMEM((2, CHUNKS, 64, 128), jnp.float32),
            pltpu.VMEM((256, 512), jnp.float32),
            pltpu.VMEM((256, 128), jnp.float32),
            pltpu.VMEM((32, 8, 512), jnp.float32),
            pltpu.VMEM((PAIRS, 8, 256), jnp.float32),
            pltpu.VMEM((128, 512), jnp.float32),
            pltpu.VMEM((128, 128), jnp.float32),
            pltpu.VMEM((16, 8, 512), jnp.float32),
            pltpu.VMEM((16, 8, 128), jnp.float32),
            pltpu.VMEM((128, 512), jnp.float32),
            pltpu.VMEM((128, 128), jnp.float32),
            dma((6,)), dma((3, 2, CHUNKS)), dma((2, CHUNKS)), dma((2, 2)), dma((2, 2, 16)), dma((2, 2, 16)),
        ],
        compiler_params=pltpu.CompilerParams(collective_id=0, has_side_effects=True),
    )(tiles, mask.T, dest.T)


def solution(mesh):
    in_specs = (
        P(("leaf", "row"), None, "col"),
        P(("leaf", "row"), "col"),
        P(("leaf", "row"), None),
    )
    return jax.shard_map(
        per_device, mesh=mesh, in_specs=in_specs, out_specs=P("leaf", None, "col"), check_vma=False
    )
```

```python
import functools

import jax
import jax.numpy as jnp
from jax import lax
from jax.experimental import pallas as pl
from jax.experimental.pallas import tpu as pltpu
from jax.sharding import PartitionSpec as P

MESH = pl.DeviceIdType.MESH
HIGH = lax.Precision.HIGHEST
EDGE = 64
PAIRS = 8
CHUNKS = 16
LAG = 8
FAR_FIRST = (8, 7, 9, 6, 10, 5, 11, 4, 12, 3, 13, 2, 14, 1, 15)


def split_dot(a, b):
    a_high, b_high = a.astype(jnp.bfloat16), b.astype(jnp.bfloat16)
    a_low = (a - a_high.astype(jnp.float32)).astype(jnp.bfloat16)
    b_low = (b - b_high.astype(jnp.float32)).astype(jnp.bfloat16)
    dot = functools.partial(jnp.dot, preferred_element_type=jnp.float32)
    return dot(a_high, b_high) + (dot(a_low, b_high) + dot(a_high, b_low))


def gather_kernel(tiles, mask_in, dest_in, out, mask, dest, wide, pan, acc, gram, got, front, part, part_g, come, come_g, full, full_g, load_sem, send_sem, recv_sem, leaf_sem, rs_sem, ag_sem):
    leaf = lax.axis_index("leaf")
    row = lax.axis_index("row")
    col = lax.axis_index("col")
    y = col // 2
    mine = col % 2
    other = 1 - mine
    rows_n = lax.axis_size("row")

    def at(y_to, x_to):
        return (leaf, row, lax.rem(y_to + 4, 4) * 2 + x_to)

    up, down, across = at(y + 1, mine), at(y - 1, mine), at(y, other)
    middle = at(2, mine)
    peer = lambda j: (leaf, lax.rem(row + j, rows_n), col)
    partner = (1 - leaf, row, col)

    lanes = 128
    loads = []
    for b in range(4):
        span = pl.ds(b * lanes, lanes)
        loads.append(pltpu.make_async_copy(tiles.at[:, :, span], wide.at[:, :, span], load_sem.at[b]))
    loads[0].start()

    small = [pltpu.make_async_copy(mask_in, mask, load_sem.at[4]), pltpu.make_async_copy(dest_in, dest, load_sem.at[5])]
    for cp in small:
        cp.start()

    barrier = pltpu.get_barrier_semaphore()
    targets = [up, down, across, partner] + [peer(j) for j in range(1, 16)]
    for t in targets:
        pl.semaphore_signal(barrier, inc=1, device_id=t, device_id_type=MESH)

    def blocks_of(rows_, width):
        shape = (rows_, width)
        return (lax.broadcasted_iota(jnp.int32, shape, 1) // EDGE == lax.broadcasted_iota(jnp.int32, shape, 0)).astype(jnp.float32)

    for cp in small:
        cp.wait()
    maskw = lax.dot_general(mask[...].astype(jnp.float32), blocks_of(8, 512), (((0,), (0,)), ((), ())), preferred_element_type=jnp.float32)
    in_first = jnp.broadcast_to((dest[...] < 16).astype(jnp.float32), (8, 32))
    first = jnp.dot(in_first, blocks_of(32, 2048), preferred_element_type=jnp.float32)
    for k in range(PAIRS):
        front[k] = first[:, k * 256:(k + 1) * 256]
    for t in range(32):
        got[t] = jnp.broadcast_to(maskw[t:t + 1], (8, 512))

    def copy_of(p, c, way, to):
        return pltpu.make_async_remote_copy(
            src_ref=pan.at[p, c], dst_ref=pan.at[p, c], send_sem=send_sem.at[way, p, c],
            recv_sem=recv_sem.at[p, c], device_id=to, device_id_type=MESH)

    edge_y = y == 0
    relay_y = lax.rem(y, 2) == 1

    def sends(c, act):
        half = jnp.logical_and(relay_y, lax.rem(c, 2) == y // 2)

        act(copy_of(mine, c, 0, across))

        @pl.when(edge_y)
        def _():
            act(copy_of(mine, c, 1, up))
            act(copy_of(mine, c, 2, down))

        @pl.when(half)
        def _():
            act(copy_of(mine, c, 1, middle))

    for b in range(1, 4):
        loads[b].start()
    start = lambda cp: cp.start()
    drain = lambda cp: cp.wait_send()

    loads[0].wait()
    pl.semaphore_wait(barrier, len(targets))

    @pl.when(y == 0)
    def _():
        def pack(c, carry):
            two = [wide[2 * c + t, :, 0:lanes] * got[2 * c + t, 0:1, 0:lanes] for t in range(2)]
            pan[mine, c] = jnp.concatenate(two, axis=0).T[0:EDGE, :]
            sends(c, start)
            return carry

        lax.fori_loop(0, CHUNKS, pack, 0)

    acc[...] = jnp.zeros_like(acc)
    gram[...] = jnp.zeros_like(gram)

    def step_fn(i, carry):
        @pl.when(i == LAG)
        def _():
            for b in range(1, 4):
                loads[b].wait()

        @pl.when(jnp.logical_and(i < CHUNKS, y > 0))
        def _():
            copy_of(mine, i, 0, up).wait_recv()
            sends(i, start)

        @pl.when(i >= LAG)
        def _():
            c = i - LAG

            copy_of(other, c, 0, up).wait_recv()

        @pl.when(jnp.logical_and(i >= LAG, lax.rem(i - LAG, 2) == 1))
        def _():
            k = (i - LAG) // 2
            right = []
            for t in range(4):
                tile = 4 * k + t
                right.append(wide[tile] * got[tile, 0:1, :])
            right = jnp.concatenate(right, axis=0)
            left = jnp.concatenate(
                [jnp.concatenate([pan[p, 2 * k], pan[p, 2 * k + 1]], axis=1) for p in range(2)], axis=0)
            sel = front[k, 0:1, :]
            both = jnp.concatenate([left * sel, left * (1.0 - sel)], axis=0)
            gram[...] += lax.dot_general(both, left, (((1,), (1,)), ((), ())), precision=HIGH, preferred_element_type=jnp.float32)
            acc[...] += split_dot(both, right)

        return carry

    lax.fori_loop(0, CHUNKS + LAG, step_fn, 0)

    other_rows = pl.ds(pl.multiple_of((1 - leaf) * 128, 128), 128)
    own_rows = pl.ds(pl.multiple_of(leaf * 128, 128), 128)
    slot = pl.ds(pl.multiple_of(row * 8, 8), 8)

    def remote(src, dst, sems, n, to):
        cp = pltpu.make_async_remote_copy(
            src_ref=src, dst_ref=dst, send_sem=sems.at[(0,) + n], recv_sem=sems.at[(1,) + n], device_id=to, device_id_type=MESH)
        cp.start()
        return cp

    sums = [gram, acc]
    parts = [part_g, part]
    comes = [come_g, come]
    fulls = [full_g, full]
    gives = [remote(sums[t].at[other_rows], parts[t], leaf_sem, (t,), partner) for t in range(2)]

    def piece(j):
        return pl.ds(pl.multiple_of(leaf * 128 + lax.rem(row + j, rows_n) * 8, 8), 8)

    scats = []
    for t in range(2):
        gives[t].wait_recv()
        sums[t][own_rows] = sums[t][own_rows] + parts[t][...]
        scats.append([remote(sums[t].at[piece(j)], comes[t].at[j], rs_sem, (t, j), peer(j)) for j in FAR_FIRST])
    spreads = []
    for t in range(2):
        for cp in scats[t]:
            cp.wait_recv()
        total = sums[t][piece(0)]
        for j in range(1, 16):
            total = total + comes[t][j]
        fulls[t][slot] = total
        spreads.append([remote(fulls[t].at[slot], fulls[t].at[slot], ag_sem, (t, j), peer(j)) for j in FAR_FIRST])

    def finish(c, carry):
        sends(c, drain)
        return carry

    lax.fori_loop(0, CHUNKS, finish, 0)
    for cp in gives + scats[0] + scats[1]:
        cp.wait_send()
    for cp in spreads[0]:
        cp.wait_recv()
    low = inverse_of_factor(full_g[...])
    for cp in spreads[0]:
        cp.wait_send()
    line = lax.broadcasted_iota(jnp.int32, (128, 512), 0) // EDGE
    place = (lax.broadcasted_iota(jnp.int32, (128, 512), 1) // EDGE) * 8 + col
    for cp in spreads[1]:
        cp.wait_recv()
    top = jnp.dot(low, full[...], precision=HIGH, preferred_element_type=jnp.float32)
    out[0] = jnp.where(place >= line, top, 0.0)

    for cp in spreads[1]:
        cp.wait_send()


def inverse_lower(d):
    n = d.shape[0]
    lane = lax.broadcasted_iota(jnp.int32, (n, 128), 1)
    line = lax.broadcasted_iota(jnp.int32, (n, 128), 0)
    cols = [jnp.broadcast_to(d[:, k:k + 1], (n, 128)) for k in range(n)]
    x = (lane == line).astype(jnp.float32)
    pivots = jnp.ones((n, 128), jnp.float32)
    for j in range(n):
        pivot = cols[j][j:j + 1, :]
        m = jnp.where(line > j, cols[j] * (1.0 / pivot), 0.0)
        for k in range(j + 1, n):
            cols[k] = cols[k] - m * cols[k][j:j + 1, :]
        x = x - m * x[j:j + 1, :]
        pivots = jnp.where(line == j, pivot, pivots)
    return (x / jnp.sqrt(pivots))[:, 0:n]


def inverse_of_factor(g):
    n = 32
    size = g.shape[0]
    eye = (lax.broadcasted_iota(jnp.int32, g.shape, 0) == lax.broadcasted_iota(jnp.int32, g.shape, 1)).astype(jnp.float32)
    rest = jnp.concatenate([eye, g], axis=1)
    done = []
    for b in range(size // n):
        at = size + b * n
        low = inverse_lower(rest[0:n, at:at + n])
        lead = jnp.dot(low, rest[0:n], precision=HIGH, preferred_element_type=jnp.float32)
        done.append(lead[:, 0:size])
        if b + 1 < size // n:
            left = lead[:, at + n:2 * size]
            rest = rest[n:] - lax.dot_general(left, lead, (((0,), (0,)), ((), ())), precision=HIGH, preferred_element_type=jnp.float32)
    return jnp.concatenate(done, axis=0)


def per_device(tiles, mask, dest):
    vmem = pl.BlockSpec(memory_space=pltpu.VMEM)
    dma = pltpu.SemaphoreType.DMA
    return pl.pallas_call(
        gather_kernel,
        out_shape=jax.ShapeDtypeStruct((1, 128, 512), jnp.float32),
        in_specs=[pl.BlockSpec(memory_space=pl.ANY)] * 3,
        out_specs=vmem,
        scratch_shapes=[
            pltpu.VMEM((8, 32), jnp.int32),
            pltpu.VMEM((1, 32), jnp.int32),
            pltpu.VMEM((32, 64, 512), jnp.float32),
            pltpu.VMEM((2, CHUNKS, 64, 128), jnp.float32),
            pltpu.VMEM((256, 512), jnp.float32),
            pltpu.VMEM((256, 128), jnp.float32),
            pltpu.VMEM((32, 8, 512), jnp.float32),
            pltpu.VMEM((PAIRS, 8, 256), jnp.float32),
            pltpu.VMEM((128, 512), jnp.float32),
            pltpu.VMEM((128, 128), jnp.float32),
            pltpu.VMEM((16, 8, 512), jnp.float32),
            pltpu.VMEM((16, 8, 128), jnp.float32),
            pltpu.VMEM((128, 512), jnp.float32),
            pltpu.VMEM((128, 128), jnp.float32),
            dma((6,)), dma((3, 2, CHUNKS)), dma((2, CHUNKS)), dma((2, 2)), dma((2, 2, 16)), dma((2, 2, 16)),
        ],
        compiler_params=pltpu.CompilerParams(collective_id=0, has_side_effects=True),
    )(tiles, mask.T, dest.T)


def solution(mesh):
    in_specs = (
        P(("leaf", "row"), None, "col"),
        P(("leaf", "row"), "col"),
        P(("leaf", "row"), None),
    )
    return jax.shard_map(
        per_device, mesh=mesh, in_specs=in_specs, out_specs=P("leaf", None, "col"), check_vma=False
    )
```
